128 devices in a mesh: section: 4 (over z), seq: 16 (over x_hi, y, core), dp: 2 (over x_lo).
Axes of the slice: x: 4 (x_hi: 2, x_lo: 2; x = x_hi * 2 + x_lo), y: 4, z: 4, core: 2. Of those that a mesh axis runs over, the one named last changes fastest.
Arguments:
- layer_input: bfloat16 [4, 2, 2048, 2048], P('section', 'dp', 'seq'), may hold values from -6 to 6
- tangent_input: bfloat16 [4, 2, 2048, 2048], P('section', 'dp', 'seq'), may hold values from -6 to 6
- cotangent_input: bfloat16 [4, 2, 2048, 2048], P('section', 'dp', 'seq'), may hold values from -6 to 6
- saved_normed: bfloat16 [4, 2, 2048, 2048], P('section', 'dp'), may hold values from -6 to 6
- saved_inv_rms: float32 [4, 2, 2048], P('section', 'dp', 'seq'), may hold values from 0.5 to 2
- saved_projections: bfloat16 [4, 2, 2048, 16, 384], P('section', 'dp', None, 'seq'), may hold values from -6 to 6
- time_index: int32 [4, 2, 2], P('section', 'dp'), may hold values from 0 to 999
- input_weight: bfloat16 [4, 2048, 16, 384], P('section', None, 'seq'), may hold values from -3 to 3
- output_weight: bfloat16 [4, 16, 128, 2048], P('section'), may hold values from -0.125 to 0.125
- norm_gain: float32 [4, 2048], P('section'), may hold values from 0.5 to 1.5
- time_scale: float32 [4, 2048], P('section'), may hold values from -0.3 to 0.3
Outputs:
- next_input: bfloat16 [4, 2, 2048, 2048], P('section', 'dp', 'seq')
- next_tangent: bfloat16 [4, 2, 2048, 2048], P('section', 'dp', 'seq')
- prev_cotangent: bfloat16 [4, 2, 2048, 2048], P('section', 'dp', 'seq')
- input_weight_gradient: float32 [4, 2048, 16, 384], P('section', 'dp', 'seq')
- output_weight_gradient: float32 [4, 16, 128, 2048], P('section', 'seq', None, 'dp')
- modulation_gradient: float32 [4, 2, 2048], P('section')
The draws below stay inside these ranges and needn't reach their ends.
Inputs may be any that keep to these rules, and one draw needn't show every extreme that they name: `time_index`: index 0 of the last dimension is the forward micro-batch's, 1 the backward micro-batch's.
All inputs are finite; a program needn't handle non-finite values.
Results may differ from the reference program's by a relative error of at most 0.014.
Values may be sent and summed in bfloat16 or wider, within the bound.
No kernel may reach another device: no remote copies, remote signals or barrier semaphores. Data moves between devices by JAX's collectives and lax.ppermute only.
A program may use at most 128 MiB of HBM per device.

```python
import math
import jax
import jax.numpy as jnp
from jax import lax

D = 2048
HD = 128
TSTEPS = 1000
TOKENS = 2048
HEADS = 16
N_SECTION = 4
N_DP = 2


def paired_rows(key, salt_value):
    drawn = jax.random.truncated_normal(jax.random.fold_in(key, salt_value), -6.0, 6.0, (N_SECTION * N_DP, TOKENS, D), jnp.float32)
    return drawn.reshape(N_SECTION, N_DP, TOKENS, D).astype(jnp.bfloat16)


def draw_layer_input(key, part):
    return paired_rows(key, 101)


def draw_tangent_input(key, part):
    return paired_rows(key, 202)


def draw_saved_projections(key, part):
    drawn = jax.random.truncated_normal(jax.random.fold_in(key, 31), -6.0, 6.0, (N_SECTION, N_DP, TOKENS, HEADS, 3 * HD), jnp.float32)
    return drawn.astype(jnp.bfloat16)


def draw_input_weight(key, part):
    drawn = jax.random.truncated_normal(jax.random.fold_in(key, 53), -4.0, 4.0, (N_SECTION, D, HEADS, 3 * HD), jnp.float32) * D ** (-0.5)
    return drawn.astype(jnp.bfloat16)


def plant(array, rng, low, largest):
    longest = array.shape.index(max(array.shape))
    spots = []
    for shift in (0, 1):
        where = [jax.random.randint(jax.random.fold_in(rng, axis), (), 0, length) for axis, length in enumerate(array.shape)]
        where[longest] = (where[longest] + shift) % array.shape[longest]
        spots.append(tuple(where))
    return array.at[spots[0]].set(low).at[spots[1]].set(largest)


def block_scale(key, dims, pieces, smallest, top_value):
    def one(position, blocks):
        steps = jax.random.uniform(jax.random.fold_in(jax.random.fold_in(key, 6), position), (blocks,), jnp.float32, smallest / len(pieces), top_value / len(pieces))
        return jnp.repeat(jnp.exp(steps), dims[position] // blocks).reshape((-1,) + (1,) * (len(dims) - position - 1))

    factor_of = one(*pieces[0])
    for cut in pieces[1:]:
        factor_of = factor_of * one(*cut)
    return factor_of


def scatter_about(rng, shape, scale, reach, pieces=(), kind=jnp.bfloat16):
    values = scale * jax.random.normal(rng, shape, jnp.float32)
    if pieces:
        values = values * block_scale(rng, shape, pieces, -0.22, 0.18)
    return jnp.clip(values, -reach, reach).astype(kind)


def setup_inputs(seed: int = 0) -> dict:
    seeds = jax.random.split(jax.random.key(seed), 12)
    return {
        "layer_input": draw_layer_input(jax.random.fold_in(seeds[11], 71), 0),
        "tangent_input": draw_tangent_input(jax.random.fold_in(seeds[11], 71), 0),
        "cotangent_input": scatter_about(seeds[2], (N_SECTION, N_DP, TOKENS, D), 1.0, 6.0, ((0, 4), (1, 2), (2, 16))),
        "saved_normed": scatter_about(seeds[3], (N_SECTION, N_DP, TOKENS, D), 1.0, 6.0, ((0, 4), (1, 2))),
        "saved_inv_rms": jnp.clip(jnp.exp(math.log(2.0) - 1.3862944 * jax.random.uniform(seeds[4], (N_SECTION, N_DP, TOKENS), jnp.float32) ** block_scale(seeds[4], (N_SECTION, N_DP, TOKENS), ((0, 4), (1, 2), (2, 16)), -0.2, 0.2)), 0.5, 2.0),
        "saved_projections": draw_saved_projections(jax.random.fold_in(seeds[11], 71), 0),
        "time_index": plant(jax.random.randint(seeds[6], (N_SECTION, N_DP, 2), 0, TSTEPS), jax.random.fold_in(seeds[6], 1), 0, TSTEPS - 1).astype(jnp.int32),
        "input_weight": draw_input_weight(jax.random.fold_in(seeds[11], 71), 0),
        "output_weight": scatter_about(seeds[8], (N_SECTION, HEADS, HD, D), (HEADS * HD) ** -0.5, 0.125, ((0, 4),)),
        "norm_gain": jnp.clip(1.0 + 0.1 * jax.random.normal(seeds[9], (N_SECTION, D), jnp.float32), 0.5, 1.5),
        "time_scale": jnp.clip(jax.random.uniform(seeds[10], (N_SECTION, D), jnp.float32, -0.3, 0.3) * block_scale(seeds[10], (N_SECTION, D), ((0, 4),), -0.4, 0.0), -0.3, 0.3),
    }


EPS = 1e-06

def timesteps(indices):
    return math.pi / 2 * (indices.astype(jnp.float32) + 0.5) / TSTEPS

def attend_tangent(queries, keys, values, tan_queries, tan_keys, tan_values):
    rows = queries.shape[0]
    block_rows = min(512, rows)
    scale = 1.0 / math.sqrt(queries.shape[1])

    def one_block(inputs):
        query_block, tangent_block = inputs
        scores = jnp.einsum('qd,kd->qk', query_block, keys, preferred_element_type=jnp.float32) * scale
        probs = jax.nn.softmax(scores, axis=-1)
        tan_scores = (jnp.einsum('qd,kd->qk', tangent_block, keys, preferred_element_type=jnp.float32) + jnp.einsum('qd,kd->qk', query_block, tan_keys, preferred_element_type=jnp.float32)) * scale
        tan_probs = probs * (tan_scores - lax.optimization_barrier(jnp.sum(probs * tan_scores, -1, keepdims=True)))
        probs_low = probs.astype(jnp.bfloat16)
        tan_low = tan_probs.astype(jnp.bfloat16)
        attended = jnp.dot(probs_low, values, preferred_element_type=jnp.float32)
        tan_attended = jnp.dot(tan_low, values, preferred_element_type=jnp.float32) + jnp.dot(probs_low, tan_values, preferred_element_type=jnp.float32)
        return (attended.astype(jnp.bfloat16), tan_attended.astype(jnp.bfloat16))
    shaped = (queries.reshape(rows // block_rows, block_rows, -1), tan_queries.reshape(rows // block_rows, block_rows, -1))
    attended, tan_attended = lax.map(one_block, shaped)
    return (attended.reshape(rows, -1), tan_attended.reshape(rows, -1))

def attend_backward(queries, keys, values, grad_attended):
    rows, head_size = queries.shape
    block_rows = min(512, rows)
    scale = 1.0 / math.sqrt(head_size)

    def one_block(carry, inputs):
        grad_keys, grad_values = carry
        query_block, grad_block = inputs
        scores = jnp.einsum('qd,kd->qk', query_block, keys, preferred_element_type=jnp.float32) * scale
        probs = jax.nn.softmax(scores, axis=-1)
        probs_low = probs.astype(jnp.bfloat16)
        attended = jnp.dot(probs_low, values, preferred_element_type=jnp.float32).astype(jnp.bfloat16)
        grad_values = grad_values + jnp.einsum('qk,qd->kd', probs_low, grad_block, preferred_element_type=jnp.float32)
        grad_probs = jnp.einsum('qd,kd->qk', grad_block, values, preferred_element_type=jnp.float32)
        grad_scores = probs * (grad_probs - lax.optimization_barrier(jnp.sum(probs * grad_probs, -1, keepdims=True))) * scale
        grad_low = grad_scores.astype(jnp.bfloat16)
        grad_queries = jnp.dot(grad_low, keys, preferred_element_type=jnp.float32)
        grad_keys = grad_keys + jnp.einsum('qk,qd->kd', grad_low, query_block, preferred_element_type=jnp.float32)
        return ((grad_keys, grad_values), (grad_queries, attended))
    zeros = jnp.zeros((rows, head_size), jnp.float32)
    shaped = (queries.reshape(rows // block_rows, block_rows, head_size), grad_attended.reshape(rows // block_rows, block_rows, head_size))
    (grad_keys, grad_values), (grad_queries, attended) = lax.scan(one_block, (zeros, zeros), shaped)
    return (grad_queries.reshape(rows, head_size), grad_keys, grad_values, attended.reshape(rows, head_size))

def reference(layer_input, tangent_input, cotangent_input, saved_normed, saved_inv_rms, saved_projections, time_index, input_weight, output_weight, norm_gain, time_scale):
    width = input_weight.shape[1]
    heads = input_weight.shape[2]
    head_size = input_weight.shape[3] // 3
    total = layer_input.shape[2]
    outputs_fwd = []
    tangents_fwd = []
    cotangents = []
    qkv_grads = []
    out_grads = []
    mod_grads = []
    for section_num in range(N_SECTION):
        weight_heads = input_weight[section_num]
        output_flat = output_weight[section_num].reshape(heads * head_size, width)
        section_outputs = []
        section_tangents = []
        section_cots = []
        qkv_sum = jnp.zeros((heads, width, 3 * head_size), jnp.float32)
        out_sum = jnp.zeros((heads, head_size, width), jnp.float32)
        mod_sum = jnp.zeros((2, width), jnp.float32)
        for clip_num in range(N_DP):
            times = timesteps(time_index[section_num, clip_num])
            hidden = layer_input[section_num, clip_num].astype(jnp.float32)
            tangent = tangent_input[section_num, clip_num].astype(jnp.float32)
            inverse = lax.rsqrt(lax.optimization_barrier(jnp.mean(hidden * hidden, -1, keepdims=True)) + EPS)
            normal = hidden * inverse
            tan_inverse = -inverse ** 3 * lax.optimization_barrier(jnp.mean(hidden * tangent, -1, keepdims=True))
            tan_normal = tangent * inverse + hidden * tan_inverse
            modulated = norm_gain[section_num] + jnp.sin(times[0]) * time_scale[section_num]
            tan_modulated = jnp.cos(times[0]) * time_scale[section_num]
            normed = (normal * modulated).astype(jnp.bfloat16)
            tan_normed = (tan_normal * modulated + normal * tan_modulated).astype(jnp.bfloat16)
            stacked = jnp.stack([normed, tan_normed])
            projected = jnp.einsum('srd,dc->src', stacked, weight_heads.reshape(width, heads * 3 * head_size), preferred_element_type=jnp.float32).astype(jnp.bfloat16)
            projected = projected.reshape(2, total, heads, 3 * head_size).transpose(2, 0, 1, 3)

            def head_forward(group_in):
                return attend_tangent(group_in[0, :, :head_size], group_in[0, :, head_size:2 * head_size], group_in[0, :, 2 * head_size:], group_in[1, :, :head_size], group_in[1, :, head_size:2 * head_size], group_in[1, :, 2 * head_size:])
            attended, tan_attended = lax.map(head_forward, projected)
            attended = attended.transpose(1, 0, 2).reshape(total, heads * head_size)
            tan_attended = tan_attended.transpose(1, 0, 2).reshape(total, heads * head_size)
            section_outputs.append((hidden + jnp.dot(attended, output_flat, preferred_element_type=jnp.float32)).astype(jnp.bfloat16))
            section_tangents.append((tangent + jnp.dot(tan_attended, output_flat, preferred_element_type=jnp.float32)).astype(jnp.bfloat16))
            cot_rows = cotangent_input[section_num, clip_num]
            normed_all = saved_normed[section_num, clip_num]

            def head_backward(carry, inputs):
                saved_head, out_head, weight_head = inputs
                grad_out = jnp.einsum('td,hd->th', cot_rows, out_head, preferred_element_type=jnp.float32).astype(jnp.bfloat16)
                grad_q, grad_k, grad_v, attended_b = attend_backward(saved_head[:, :head_size], saved_head[:, head_size:2 * head_size], saved_head[:, 2 * head_size:], grad_out)
                out_grad = jnp.einsum('th,td->hd', attended_b, cot_rows, preferred_element_type=jnp.float32)
                grad_proj = jnp.concatenate([grad_q, grad_k, grad_v], -1).astype(jnp.bfloat16)
                qkv_grad = jnp.einsum('td,tc->dc', normed_all, grad_proj, preferred_element_type=jnp.float32)
                term = jnp.einsum('tc,dc->td', grad_proj, weight_head, preferred_element_type=jnp.float32).astype(jnp.bfloat16)
                term = lax.optimization_barrier(term)
                return (carry + term.astype(jnp.float32), (qkv_grad, out_grad))
            start = jnp.zeros((total, width), jnp.float32)
            grad_normed, (qkv_part, out_part) = lax.scan(head_backward, start, (saved_projections[section_num, clip_num].transpose(1, 0, 2), output_weight[section_num], weight_heads.transpose(1, 0, 2)))
            modulated_b = norm_gain[section_num] + jnp.sin(times[1]) * time_scale[section_num]
            normal_b = normed_all.astype(jnp.float32) / modulated_b
            weighted = grad_normed * modulated_b
            grad_hidden = saved_inv_rms[section_num, clip_num][:, None] * (weighted - normal_b * lax.optimization_barrier(jnp.mean(normal_b * weighted, -1, keepdims=True)))
            section_cots.append((cot_rows.astype(jnp.float32) + grad_hidden).astype(jnp.bfloat16))
            gain_part = lax.optimization_barrier(jnp.sum(grad_normed * normal_b, 0))
            mod_sum = mod_sum + jnp.stack([gain_part, jnp.sin(times[1]) * gain_part])
            qkv_sum = qkv_sum + qkv_part
            out_sum = out_sum + out_part
        outputs_fwd.append(jnp.stack(section_outputs))
        tangents_fwd.append(jnp.stack(section_tangents))
        cotangents.append(jnp.stack(section_cots))
        qkv_grads.append(qkv_sum.transpose(1, 0, 2))
        out_grads.append(out_sum)
        mod_grads.append(mod_sum)
    next_input = jnp.roll(jnp.stack(outputs_fwd), 1, axis=0)
    next_tangent = jnp.roll(jnp.stack(tangents_fwd), 1, axis=0)
    prev_cotangent = jnp.roll(jnp.stack(cotangents), -1, axis=0)
    return (next_input, next_tangent, prev_cotangent, jnp.stack(qkv_grads), jnp.stack(out_grads), jnp.stack(mod_grads))
```

```python
import math

import jax
import jax.numpy as jnp
from jax import lax
from jax.experimental import pallas as pl
from jax.experimental.pallas import tpu as pltpu
from jax.sharding import PartitionSpec as P

TSTEPS = 1000
EPS = 1e-06
LOG2E = math.log2(math.e)
F32 = jnp.float32
BF = jnp.bfloat16
NN = (((1,), (0,)), ((), ()))
NT = (((1,), (1,)), ((), ()))
TN = (((0,), (0,)), ((), ()))
VMEM_LIMIT = 48 << 20


NX, NY, NC = 2, 4, 2


def place(x, y, core):
    return (x * NY + y) * NC + core


def pairs(move):
    spots = [(x, y, c) for x in range(NX) for y in range(NY) for c in range(NC)]
    return [(place(*spot), place(*move(*spot))) for spot in spots]


def along_y(steps):
    return pairs(lambda x, y, c: (x, (y + steps) % NY, c))


ACROSS_X = pairs(lambda x, y, c: (1 - x, y, c))
ACROSS_CORE = pairs(lambda x, y, c: (x, y, 1 - c))
SAME_CORE = [[place(x, y, c) for x in range(NX) for y in range(NY)] for c in range(NC)]


def send(value, route):
    return lax.ppermute(value, "seq", route)


def passed_along(value, axis, steps):
    count = lax.axis_size(axis)
    return lax.ppermute(value, axis, [(source, (source + steps) % count) for source in range(count)])


def timesteps(indices):
    return math.pi / 2 * (indices.astype(F32) + 0.5) / TSTEPS


def dotf(a, b, dims=NN):
    return lax.dot_general(a, b, dims, preferred_element_type=F32)


def params(*semantics):
    return pltpu.CompilerParams(vmem_limit_bytes=VMEM_LIMIT)


def attend_forward(proj, where):
    _, _, half, cols = proj.shape
    hs = cols // 3
    bq = 128
    steps = half // bq
    scale = 1.0 / math.sqrt(hs)

    def kernel(where_ref, q_ref, all_ref, out_ref, kcat, vcat):
        @pl.when(pl.program_id(0) == 0)
        def _():
            for j in range(2):
                for st in range(2):
                    rows = slice(j * half, (j + 1) * half)
                    at = slice(st * hs, (st + 1) * hs)
                    kcat[rows, at] = all_ref[j, st, :, hs : 2 * hs]
                    vcat[rows, at] = all_ref[j, st, :, 2 * hs :]

        q = jnp.concatenate([q_ref[0, 0, :, :hs], q_ref[1, 0, :, :hs]], 0)
        tq = jnp.concatenate([q_ref[0, 1, :, :hs], q_ref[1, 1, :, :hs]], 0)
        s = dotf(q, kcat[:, :hs], NT)
        ts = dotf(jnp.concatenate([tq, q], 1), kcat[...], NT)
        top = jnp.max(s, -1, keepdims=True)
        e = jnp.exp2((s - top) * (scale * LOG2E))
        r = 1.0 / jnp.sum(e, -1, keepdims=True)
        t = jnp.sum(e * ts, -1, keepdims=True) * r
        w = (e * (ts - t)).astype(BF)
        pv = dotf(e.astype(BF), vcat[...])
        tv = dotf(w, vcat[:, :hs])
        primal = (pv[:, :hs] * r).astype(BF)
        tangent = ((tv * scale + pv[:, hs:]) * r).astype(BF)
        own = where_ref[steps]
        for j, slot in ((0, own), (1, 1 - own)):
            out_ref[slot, 0] = primal[j * bq : (j + 1) * bq]
            out_ref[slot, 1] = tangent[j * bq : (j + 1) * bq]

    return pl.pallas_call(
        kernel,
        out_shape=jax.ShapeDtypeStruct((2 * steps, 2, bq, hs), BF),
        grid_spec=pltpu.PrefetchScalarGridSpec(
            num_scalar_prefetch=1,
            grid=(steps,),
            in_specs=[
                pl.BlockSpec((2, 2, bq, cols), lambda i, w: (0, 0, i, 0)),
                pl.BlockSpec((2, 2, half, cols), lambda i, w: (0, 0, 0, 0)),
            ],
            out_specs=pl.BlockSpec((2, 2, bq, hs), lambda i, w: (w[i], 0, 0, 0)),
            scratch_shapes=[pltpu.VMEM((2 * half, 2 * hs), BF), pltpu.VMEM((2 * half, 2 * hs), BF)],
        ),
        compiler_params=params(),
        name="attend_forward",
    )(where, proj, proj)


def attend_backward(saved, grad):
    rows, cols = saved.shape
    hs = cols // 3
    bq = 256
    steps = rows // bq
    scale = 1.0 / math.sqrt(hs)

    def kernel(saved_ref, g_ref, att_ref, dproj_ref, dk, dv):
        i = pl.program_id(0)

        @pl.when(i == 0)
        def _():
            dk[...] = jnp.zeros_like(dk)
            dv[...] = jnp.zeros_like(dv)

        k = saved_ref[:, hs : 2 * hs]
        v = saved_ref[:, 2 * hs :]
        at = pl.ds(pl.multiple_of(i * bq, bq), bq)
        q = saved_ref[at, :hs]
        do = g_ref[...]
        s = dotf(q, k, NT)
        dp = dotf(do, v, NT)
        top = jnp.max(s, -1, keepdims=True)
        e = jnp.exp2((s - top) * (scale * LOG2E))
        p = e * (1.0 / jnp.sum(e, -1, keepdims=True))
        pb = p.astype(BF)
        delta = jnp.sum(p * dp, -1, keepdims=True)
        ds = (p * (dp - delta)).astype(BF)
        att_ref[...] = dotf(pb, v).astype(BF)
        dproj_ref[at, :hs] = (dotf(ds, k) * scale).astype(BF)
        dv[...] += dotf(pb, do, TN)
        dk[...] += dotf(ds, q, TN)

        @pl.when(i == steps - 1)
        def _():
            dproj_ref[:, hs : 2 * hs] = (dk[...] * scale).astype(BF)
            dproj_ref[:, 2 * hs :] = dv[...].astype(BF)

    return pl.pallas_call(
        kernel,
        out_shape=(jax.ShapeDtypeStruct((rows, hs), BF), jax.ShapeDtypeStruct((rows, cols), BF)),
        grid=(steps,),
        in_specs=[pl.BlockSpec((rows, cols), lambda i: (0, 0)), pl.BlockSpec((bq, hs), lambda i: (i, 0))],
        out_specs=(pl.BlockSpec((bq, hs), lambda i: (i, 0)), pl.BlockSpec((rows, cols), lambda i: (0, 0))),
        scratch_shapes=[pltpu.VMEM((rows, hs), F32), pltpu.VMEM((rows, hs), F32)],
        compiler_params=params(),
        name="attend_backward",
    )(saved, grad)


def head_gradients(cot, output_whole):
    heads, hs, width = output_whole.shape
    rows = cot.shape[0]
    group = 4

    def kernel(g_ref, w_ref, out_ref):
        for j in range(0, group, 2):
            both = dotf(g_ref[...], w_ref[j : j + 2].reshape(2 * hs, width), NT).astype(BF)
            out_ref[j] = both[:, :hs]
            out_ref[j + 1] = both[:, hs:]

    return pl.pallas_call(
        kernel,
        out_shape=jax.ShapeDtypeStruct((heads, rows, hs), BF),
        grid=(heads // group,),
        in_specs=[
            pl.BlockSpec((rows, width), lambda i: (0, 0)),
            pl.BlockSpec((group, hs, width), lambda i: (i, 0, 0)),
        ],
        out_specs=pl.BlockSpec((group, rows, hs), lambda i: (i, 0, 0)),
        compiler_params=params(),
        name="head_gradients",
    )(cot, output_whole)


def project(pieces, weights):
    width, cols = weights.shape
    rows = sum(piece.shape[0] for piece in pieces)

    def kernel(*refs):
        ins, w_ref, own_ref, other_ref = refs[:-3], refs[-3], refs[-2], refs[-1]
        at = 0
        for ref in ins:
            n = ref.shape[0]
            both = dotf(ref[...], w_ref[...]).astype(BF)
            own_ref[at : at + n] = both[:, : cols // 2]
            other_ref[at : at + n] = both[:, cols // 2 :]
            at += n

    shape = jax.ShapeDtypeStruct((rows, cols // 2), BF)
    return pl.pallas_call(
        kernel,
        out_shape=(shape, shape),
        in_specs=[pl.BlockSpec(memory_space=pltpu.VMEM)] * (len(pieces) + 1),
        out_specs=(pl.BlockSpec(memory_space=pltpu.VMEM),) * 2,
        compiler_params=params(),
        name="project",
    )(*pieces, weights)


def back_project(mine, other, weights):
    rows, cols = mine.shape
    width = weights.shape[0]
    bm = 256

    def kernel(m_ref, o_ref, w_ref, out_ref):
        both = jnp.concatenate([m_ref[...], o_ref[...]], 1)
        out_ref[...] = dotf(both, w_ref[...], NT).astype(BF)

    return pl.pallas_call(
        kernel,
        out_shape=jax.ShapeDtypeStruct((rows, width), BF),
        grid=(rows // bm,),
        in_specs=[
            pl.BlockSpec((bm, cols), lambda i: (i, 0)),
            pl.BlockSpec((bm, cols), lambda i: (i, 0)),
            pl.BlockSpec((width, 2 * cols), lambda i: (0, 0)),
        ],
        out_specs=pl.BlockSpec((bm, width), lambda i: (i, 0)),
        compiler_params=params(),
        name="back_project",
    )(mine, other, weights)


def output_layer(moved, output_whole, hidden, tangent):
    heads, _, rows, hs = moved.shape
    width = output_whole.shape[-1]
    steps = heads // 4

    def kernel(m_ref, w_ref, h_ref, u_ref, out_ref, acc):
        i = pl.program_id(0)
        total = None
        for j in (0, 2):
            left = jnp.concatenate([m_ref[j, 0], m_ref[j, 1]], 0)
            right = jnp.concatenate([m_ref[j + 1, 0], m_ref[j + 1, 1]], 0)
            part = dotf(jnp.concatenate([left, right], 1), w_ref[j : j + 2].reshape(2 * hs, width))
            total = part if total is None else total + part

        @pl.when(i == 0)
        def _():
            acc[...] = total

        @pl.when(i > 0)
        def _():
            acc[...] += total

        @pl.when(i == steps - 1)
        def _():
            out_ref[0] = (h_ref[...].astype(F32) + acc[:rows]).astype(BF)
            out_ref[1] = (u_ref[...].astype(F32) + acc[rows:]).astype(BF)

    whole = pl.BlockSpec((rows, width), lambda i: (0, 0))
    return pl.pallas_call(
        kernel,
        out_shape=jax.ShapeDtypeStruct((2, rows, width), BF),
        grid=(steps,),
        in_specs=[
            pl.BlockSpec((4, 2, rows, hs), lambda i: (i, 0, 0, 0)),
            pl.BlockSpec((4, hs, width), lambda i: (i, 0, 0)),
            whole,
            whole,
        ],
        out_specs=pl.BlockSpec((2, rows, width), lambda i: (0, 0, 0)),
        scratch_shapes=[pltpu.VMEM((2 * rows, width), F32)],
        compiler_params=params(),
        name="output_layer",
    )(moved, output_whole, hidden, tangent)


def gather_x_first(block):
    n = block.shape[0]
    both = jnp.concatenate([block, send(block, ACROSS_X)], 0)
    below = send(both, along_y(1))
    above = send(both, along_y(-1))
    far_own = send(below[:n], along_y(1))
    far_other = send(above[n:], along_y(-1))
    return [both, below, above, far_own, far_other]


def gather_y_first(block):
    n = block.shape[0]
    below = send(block, along_y(1))
    above = send(block, along_y(-1))
    other = send(block, ACROSS_X)
    far_low = send(below[: n // 2], along_y(1))
    far_high = send(above[n // 2 :], along_y(-1))
    other_below = send(below, ACROSS_X)
    other_above = send(above, ACROSS_X)
    far = jnp.concatenate([far_low, far_high], 0)
    other_far = send(far, ACROSS_X)
    return [block, other, below, other_below, above, other_above, far, other_far]


def local(
    layer_input,
    tangent_input,
    cotangent_input,
    saved_normed,
    saved_inv_rms,
    saved_projections,
    time_index,
    input_weight,
    output_weight,
    norm_gain,
    time_scale,
):
    seq = lax.axis_index("seq")
    core = seq % NC
    dp = lax.axis_index("dp")
    weight_own = input_weight[0, :, 0, :]
    width, cols = weight_own.shape
    output_whole = output_weight[0]
    heads = output_whole.shape[0]
    gains, scales = norm_gain[0], time_scale[0]
    moments = timesteps(time_index[0, 0])
    input_rows, tangent_rows, cot_rows = layer_input[0, 0], tangent_input[0, 0], cotangent_input[0, 0]
    normed_all = saved_normed[0, 0]
    rows = cot_rows.shape[0]

    cot_all = lax.all_gather(cot_rows, "seq", axis=0, tiled=True)

    grad_out = lax.all_to_all(head_gradients(cot_rows, output_whole), "seq", 0, 0, tiled=True)
    grad_out = grad_out.reshape(heads * rows, -1)

    hidden = input_rows.astype(F32)
    tangent = tangent_rows.astype(F32)
    inverse = lax.rsqrt(jnp.mean(hidden * hidden, -1, keepdims=True) + EPS)
    normal = hidden * inverse
    tan_inverse = -(inverse**3) * jnp.mean(hidden * tangent, -1, keepdims=True)
    tan_normal = tangent * inverse + hidden * tan_inverse
    modulated = gains + jnp.sin(moments[0]) * scales
    tan_modulated = jnp.cos(moments[0]) * scales
    normed = (normal * modulated).astype(BF)
    tan_normed = (tan_normal * modulated + normal * tan_modulated).astype(BF)

    weights = jnp.concatenate([weight_own, send(weight_own, ACROSS_CORE)], 1)
    normed_pieces = gather_x_first(normed)
    tan_pieces = gather_y_first(tan_normed)

    attended_b, grad_proj = attend_backward(saved_projections[0, 0, :, 0, :], grad_out)
    by_core = grad_proj.reshape(NX * NY, NC, rows, cols)
    mine = lax.dynamic_index_in_dim(by_core, core, 1, keepdims=False).reshape(NX * NY * rows, cols)
    theirs = lax.dynamic_index_in_dim(by_core, 1 - core, 1, keepdims=False).reshape(NX * NY * rows, cols)
    other = send(theirs, ACROSS_CORE)
    terms = back_project(mine, other, weights)
    arrived = lax.all_to_all(
        terms.reshape(NX * NY, rows, width), "seq", 0, 0, axis_index_groups=SAME_CORE, tiled=True
    )

    qkv_grad = dotf(normed_all, grad_proj, TN)
    half = width // 2
    away = lax.dynamic_slice_in_dim(qkv_grad, (1 - dp) * half, half, 0).astype(BF)
    qkv_total = lax.dynamic_slice_in_dim(qkv_grad, dp * half, half, 0) + passed_along(away, "dp", 1).astype(F32)
    mod_b = gains + jnp.sin(moments[1]) * scales
    gain_part = jnp.sum(qkv_grad * weight_own.astype(F32), 1) / mod_b
    norm_part = jnp.stack([gain_part, jnp.sin(moments[1]) * gain_part])
    spread = norm_part.reshape(2, heads, -1).transpose(1, 0, 2)
    norm_sum = jnp.sum(lax.all_to_all(spread, "seq", 0, 0, tiled=True), 0)
    norm_sum = norm_sum + passed_along(norm_sum, "dp", 1)
    norm_total = lax.all_to_all(jnp.broadcast_to(norm_sum, (heads,) + norm_sum.shape), "seq", 0, 0, tiled=True)
    norm_total = norm_total.transpose(1, 0, 2).reshape(2, width)

    primal_own, primal_other = project(normed_pieces, weights)
    tan_own, tan_other = project(tan_pieces, weights)
    proj_own = jnp.stack([primal_own, tan_own])
    proj_there = send(jnp.stack([primal_other, tan_other]), ACROSS_CORE)
    x, y = seq // (NY * NC), (seq // NC) % NY
    where = [xx * NY + (y + dy) % NY for dy in (0, -1, 1, 2) for xx in (x, 1 - x)]
    where = jnp.stack(where + [core]).astype(jnp.int32)
    attended = attend_forward(jnp.stack([proj_own, proj_there]), where)
    moved = lax.all_to_all(attended, "seq", 0, 0, tiled=True)
    outgoing = output_layer(moved, output_whole, input_rows, tangent_rows)
    shifted = passed_along(outgoing, "section", 1)

    out_grad = dotf(attended_b, cot_all, TN)
    away = lax.dynamic_slice_in_dim(out_grad, (1 - dp) * half, half, 1).astype(BF)
    out_total = lax.dynamic_slice_in_dim(out_grad, dp * half, half, 1) + passed_along(away, "dp", 1).astype(F32)

    grad_normed = jnp.sum(arrived.astype(F32), 0)
    own_normed = lax.dynamic_slice_in_dim(normed_all, seq * rows, rows, 0)
    normal_b = own_normed.astype(F32) / mod_b
    weighted = grad_normed * mod_b
    grad_hidden = saved_inv_rms[0, 0][:, None] * (
        weighted - normal_b * jnp.mean(normal_b * weighted, -1, keepdims=True)
    )
    cotangent = (cot_rows.astype(F32) + grad_hidden).astype(BF)
    cot_prev = passed_along(cotangent, "section", -1)
    return (
        shifted[0][None, None],
        shifted[1][None, None],
        cot_prev[None, None],
        qkv_total[None, :, None, :],
        out_total[None, None],
        norm_total[None],
    )


def solution(mesh):
    placed = (
        P("section", "dp", "seq", None),
        P("section", "dp", "seq", None),
        P("section", "dp", "seq", None),
        P("section", "dp", None, None),
        P("section", "dp", "seq"),
        P("section", "dp", None, "seq", None),
        P("section", "dp", None),
        P("section", None, "seq", None),
        P("section", None, None, None),
        P("section", None),
        P("section", None),
    )
    return jax.shard_map(
        local,
        mesh=mesh,
        in_specs=placed,
        out_specs=(
            P("section", "dp", "seq", None),
            P("section", "dp", "seq", None),
            P("section", "dp", "seq", None),
            P("section", "dp", "seq", None),
            P("section", "seq", None, "dp"),
            P("section", None, None),
        ),
        check_vma=False,
    )
```
